32 devices in a mesh: groups: 2 (over y), seq: 4 (over z), tensor: 2 (over x), rep: 2 (over core).
Axes of the slice: x: 2, y: 2, z: 4, core: 2. Of those that a mesh axis runs over, the one named last changes fastest.
Arguments:
- hidden: bfloat16 [8192, 5376], P(('groups', 'seq'), ('tensor', 'rep')), parts along dimension 0, may hold values from -6 to 6
- frozen_query_weight: bfloat16 [8192, 2048], P(('groups', 'seq'), ('tensor', 'rep')), parts along dimension 0, may hold values from -6 to 6
- frozen_key_weight: bfloat16 [8192, 1024], P(('groups', 'seq'), ('tensor', 'rep')), parts along dimension 0, may hold values from -6 to 6
- frozen_value_weight: bfloat16 [8192, 1024], P(('groups', 'seq'), ('tensor', 'rep')), parts along dimension 0, may hold values from -6 to 6
- query_norm_offset: float32 [128], replicated, may hold values from -0.4 to 0.8
- key_norm_offset: float32 [128], replicated, may hold values from -0.4 to 0.8
- adapter_down_input: bfloat16 [4, 5376, 48], P('seq', ('tensor', 'rep')), may hold values from -0.078125 to 0.078125
- adapter_up_query: bfloat16 [4, 16, 2048], P('seq', None, ('tensor', 'rep')), may hold values from -0.359375 to 0.359375
- adapter_up_key: bfloat16 [4, 16, 1024], P('seq', None, ('tensor', 'rep')), may hold values from -0.359375 to 0.359375
- adapter_up_value: bfloat16 [4, 16, 1024], P('seq', None, ('tensor', 'rep')), may hold values from -0.359375 to 0.359375
- adapter_down_output: bfloat16 [4, 2048, 16], P('seq', ('tensor', 'rep')), may hold values from -0.125 to 0.125
- adapter_up_output: bfloat16 [4, 16, 5376], P('seq', None, ('tensor', 'rep')), may hold values from -1.5 to 1.5
- document_lengths: int32 [16], P('groups'), parts along dimension 0, may hold values from 1 to 16, 32 in all
- document_adapter_row: int32 [16, 1], P('groups'), parts along dimension 0, may hold values from 0 to 3
Outputs:
- attention: bfloat16 [8192, 2048], P(('groups', 'seq'), ('tensor', 'rep')), parts along dimension 0
- adapter_output_term: bfloat16 [8192, 5376], P(('groups', 'seq'), ('tensor', 'rep')), parts along dimension 0
The draws below stay inside these ranges and needn't reach their ends.
There are 2 independent parts, one for each index of `groups`. The reference program is written for one: setup_inputs(seed, part) draws one part's arguments, and reference() takes and returns one part's arrays. A program takes and returns all parts, laid end to end along the dimension named above; an argument that names none is the same for every part. Nothing has to cross between parts.
Inputs may be any that keep to these rules, and one draw needn't show every extreme that they name: `document_lengths`: the sizes sum to 32. `document_adapter_row`: every adapter of the pool serves at least one document.
All inputs are finite; a program needn't handle non-finite values.
Results may differ from the reference program's by a relative error of at most 0.0086.
Values may be sent and summed in bfloat16 or wider, within the bound.
No kernel may reach another device: no remote copies, remote signals or barrier semaphores. Data moves between devices by JAX's collectives and lax.ppermute only.
A program may use at most 64 MiB of HBM per device.

```python
import math
import jax
import jax.numpy as jnp
import numpy as np
from jax import lax

MODEL_WIDTH = 5376
QUERY_HEADS = 16
KEY_VALUE_HEADS = 8
HEAD_SIZE = 128
ADAPTER_RANK = 16
WINDOW_LENGTH = 1024
DOC_UNIT = 128
SLAB_TOKENS = 4096
DOCS = 8
ADAPTER_COUNT = 4
DOC_MOST = 2048


def block_levels(stream_key, extent, shards, smallest, top_value):
    factor_of = 1.0
    for dim, blocks in shards:
        steps = jax.random.uniform(jax.random.fold_in(jax.random.fold_in(stream_key, 6), dim), (blocks,), jnp.float32, smallest / len(shards), top_value / len(shards))
        factor_of = factor_of * jnp.repeat(jnp.exp(steps), extent[dim] // blocks).reshape((-1,) + (1,) * (len(extent) - 1 - dim))
    return factor_of


def picks_of(rng, rows, amount, top, lift):
    sequence = jax.random.permutation(jax.random.fold_in(rng, 1), amount)
    pull = sequence
    for power in range(3):
        pull = pull * pull // amount
    pull = pull * lift // amount
    chance = jax.random.randint(jax.random.fold_in(rng, 2), (rows, amount), 0, 4096) + pull
    fixed_rows = jax.random.permutation(jax.random.fold_in(rng, 3), rows)[jnp.arange(amount) % rows]
    chance = jnp.where(jnp.arange(rows)[:, None] == fixed_rows[None, :], 1 << 14, chance)
    merit = chance * amount + jnp.arange(amount)
    return lax.top_k(merit.astype(jnp.int32), top)[1].astype(jnp.int32)


def length_profile(count, total, bound, lean):
    portions = [(1 << 20) // math.isqrt(rank ** lean) + 1 for rank in range(2, count + 1)]
    surplus, given = total - bound - (count - 1), [1] * (count - 1)
    while surplus > 0:
        movable = [i for i in range(count - 1) if given[i] < bound]
        pool, left = sum([portions[i] for i in movable]), surplus
        for i in movable:
            extra = min(bound - given[i], max(1, left * portions[i] // pool), surplus)
            given[i] = given[i] + extra
            surplus = surplus - extra
    return np.array([bound] + given)


def uneven(key, amount, total, most, skew):
    if amount == 2:
        one = jax.random.randint(key, (), max(1, total - most), min(most, total - 1) + 1)
        return jnp.stack([one, total - one])
    tallies = jnp.asarray(length_profile(amount, total, most, skew), jnp.int32)
    couples = (amount - 1) // 2
    giver, sink = tallies[1:1 + 2 * couples:2], tallies[2:2 + 2 * couples:2]
    room = jnp.minimum(giver - 1, most - sink)
    moved = jax.random.randint(jax.random.fold_in(key, 1), (couples,), 0, 1 << 20) % (room + 1)
    tallies = tallies.at[1:1 + 2 * couples:2].set(giver - moved).at[2:2 + 2 * couples:2].set(sink + moved)
    return tallies[jax.random.permutation(jax.random.fold_in(key, 2), amount)]


def gaussian(own_key, extent, spread, limit, split=(), kind=jnp.bfloat16):
    values = spread * jax.random.normal(own_key, extent, jnp.float32)
    if split:
        values = values * block_levels(own_key, extent, split, -0.22, 0.18)
    return jnp.clip(values, -limit, limit).astype(kind)


def setup_inputs(seed: int = 0, part: int = 0) -> dict:
    arg_keys = jax.random.split(jax.random.key(seed), 15)
    part_keys = jax.random.split(jax.random.fold_in(arg_keys[14], part), 15)
    return {
        "hidden": gaussian(part_keys[0], (SLAB_TOKENS, MODEL_WIDTH), 1.0, 6.0, ((0, 4), (1, 4))),
        "frozen_query_weight": gaussian(part_keys[1], (SLAB_TOKENS, QUERY_HEADS * HEAD_SIZE), 1.0, 6.0, ((0, 4), (1, 4))),
        "frozen_key_weight": gaussian(part_keys[2], (SLAB_TOKENS, KEY_VALUE_HEADS * HEAD_SIZE), 1.0, 6.0, ((0, 4), (1, 4))),
        "frozen_value_weight": gaussian(part_keys[3], (SLAB_TOKENS, KEY_VALUE_HEADS * HEAD_SIZE), 1.0, 6.0, ((0, 4), (1, 4))),
        "query_norm_offset": jnp.clip(jax.random.uniform(arg_keys[4], (HEAD_SIZE,), jnp.float32, -0.4, 0.8), -0.4, 0.8),
        "key_norm_offset": jnp.clip(jax.random.uniform(arg_keys[5], (HEAD_SIZE,), jnp.float32, -0.4, 0.8), -0.4, 0.8),
        "adapter_down_input": gaussian(arg_keys[6], (ADAPTER_COUNT, MODEL_WIDTH, 3 * ADAPTER_RANK), MODEL_WIDTH ** -0.5, 0.078125, ((0, 4), (1, 4))),
        "adapter_up_query": gaussian(arg_keys[7], (ADAPTER_COUNT, ADAPTER_RANK, QUERY_HEADS * HEAD_SIZE), 0.06, 0.359375, ((0, 4), (2, 4))),
        "adapter_up_key": gaussian(arg_keys[8], (ADAPTER_COUNT, ADAPTER_RANK, KEY_VALUE_HEADS * HEAD_SIZE), 0.06, 0.359375, ((0, 4), (2, 4))),
        "adapter_up_value": gaussian(arg_keys[9], (ADAPTER_COUNT, ADAPTER_RANK, KEY_VALUE_HEADS * HEAD_SIZE), 0.06, 0.359375, ((0, 4), (2, 4))),
        "adapter_down_output": gaussian(arg_keys[10], (ADAPTER_COUNT, QUERY_HEADS * HEAD_SIZE, ADAPTER_RANK), (QUERY_HEADS * HEAD_SIZE) ** -0.5, 0.125, ((0, 4), (1, 4))),
        "adapter_up_output": gaussian(arg_keys[11], (ADAPTER_COUNT, ADAPTER_RANK, MODEL_WIDTH), 0.25, 1.5, ((0, 4), (2, 4))),
        "document_lengths": uneven(part_keys[12], DOCS, SLAB_TOKENS // DOC_UNIT, DOC_MOST // DOC_UNIT, 2).astype(jnp.int32),
        "document_adapter_row": picks_of(part_keys[13], DOCS, ADAPTER_COUNT, 1, 2048),
    }


ADAPTER_SCALE = 2.0
ATTN_SCALE = 168.0 ** (-0.5)
ROPE_BASE = 10000.0
NORM_EPS = 1e-06

def rotary(values, position):
    half_size = values.shape[-1] // 2
    freq_index = jnp.arange(half_size).astype(values.dtype)
    inv_freq = ROPE_BASE ** (-2.0 * freq_index / values.shape[-1])
    angles = position.astype(values.dtype)[:, None] * inv_freq[None, :]
    cosine = jnp.cos(angles)[:, None, :]
    sine_vals = jnp.sin(angles)[:, None, :]
    front_half = values[..., :half_size]
    back_half = values[..., half_size:]
    return jnp.concatenate([front_half * cosine - back_half * sine_vals, back_half * cosine + front_half * sine_vals], axis=-1)

def per_head_norm(values, offsets):
    mean_sq = lax.optimization_barrier(jnp.mean(values * values, axis=-1, keepdims=True))
    return values * lax.rsqrt(mean_sq + NORM_EPS) * (1.0 + offsets.astype(values.dtype))

def reference(hidden, frozen_query_weight, frozen_key_weight, frozen_value_weight, query_norm_offset, key_norm_offset, adapter_down_input, adapter_up_query, adapter_up_key, adapter_up_value, adapter_down_output, adapter_up_output, document_lengths, document_adapter_row):
    tok_index = jnp.arange(SLAB_TOKENS).astype(jnp.int32)
    doc_start = ((jnp.cumsum(document_lengths) - document_lengths) * DOC_UNIT).astype(jnp.int32)
    doc_of = (lax.optimization_barrier(jnp.sum((tok_index[:, None] >= doc_start[None, :]).astype(jnp.int32), axis=1)) - 1).astype(jnp.int32)
    tok_start = doc_start[doc_of]
    position = tok_index - tok_start
    adapter = document_adapter_row[:, 0][doc_of]
    tile_rows = 32

    def repeated_tiles(array):
        return array.reshape((SLAB_TOKENS // tile_rows, tile_rows) + array.shape[1:])

    def project_in(inputs):
        hidden_rows, selected_adapter = inputs
        rank_activations = jnp.einsum('ac,acz->az', hidden_rows.astype(jnp.float32), adapter_down_input[selected_adapter].astype(jnp.float32))
        rank_lower_part = lax.optimization_barrier(rank_activations.astype(jnp.bfloat16)).astype(jnp.float32)
        query_delta = jnp.einsum('xv,xvp->xp', rank_lower_part[:, 0:ADAPTER_RANK], adapter_up_query[selected_adapter].astype(jnp.float32))
        key_delta = jnp.einsum('xv,xvp->xp', rank_lower_part[:, ADAPTER_RANK:2 * ADAPTER_RANK], adapter_up_key[selected_adapter].astype(jnp.float32))
        value_delta = jnp.einsum('xv,xvp->xp', rank_lower_part[:, 2 * ADAPTER_RANK:3 * ADAPTER_RANK], adapter_up_value[selected_adapter].astype(jnp.float32))
        return (query_delta, key_delta, value_delta)
    query_delta, key_delta, value_delta = lax.map(project_in, (repeated_tiles(hidden), repeated_tiles(adapter)))
    query_rows = frozen_query_weight.astype(jnp.float32) + ADAPTER_SCALE * query_delta.reshape(SLAB_TOKENS, QUERY_HEADS * HEAD_SIZE)
    key = frozen_key_weight.astype(jnp.float32) + ADAPTER_SCALE * key_delta.reshape(SLAB_TOKENS, KEY_VALUE_HEADS * HEAD_SIZE)
    value_rows = frozen_value_weight.astype(jnp.float32) + ADAPTER_SCALE * value_delta.reshape(SLAB_TOKENS, KEY_VALUE_HEADS * HEAD_SIZE)
    query_normed = per_head_norm(query_rows.reshape(SLAB_TOKENS, QUERY_HEADS, HEAD_SIZE), query_norm_offset)
    key_after_norm = per_head_norm(key.reshape(SLAB_TOKENS, KEY_VALUE_HEADS, HEAD_SIZE), key_norm_offset)
    query_rotated = rotary(query_normed, position).astype(jnp.bfloat16)
    key_rotated = rotary(key_after_norm, position).astype(jnp.bfloat16)
    value_updated = value_rows.reshape(SLAB_TOKENS, KEY_VALUE_HEADS, HEAD_SIZE).astype(jnp.bfloat16)
    query_group_count = QUERY_HEADS // KEY_VALUE_HEADS
    query_block = min(512, SLAB_TOKENS)
    key_span = WINDOW_LENGTH + query_block
    keys_with_padding = jnp.concatenate([jnp.zeros((WINDOW_LENGTH, KEY_VALUE_HEADS, HEAD_SIZE), jnp.bfloat16), key_rotated], axis=0)
    values_with_padding = jnp.concatenate([jnp.zeros((WINDOW_LENGTH, KEY_VALUE_HEADS, HEAD_SIZE), jnp.bfloat16), value_updated], axis=0)

    def attend(row_beginning):
        query_block_rows = lax.dynamic_slice_in_dim(query_rotated, row_beginning, query_block, 0).reshape(query_block, KEY_VALUE_HEADS, query_group_count, HEAD_SIZE).astype(jnp.float32)
        block_keys = lax.dynamic_slice_in_dim(keys_with_padding, row_beginning, key_span, 0).astype(jnp.float32)
        block_values = lax.dynamic_slice_in_dim(values_with_padding, row_beginning, key_span, 0).astype(jnp.float32)
        raw_scores = jnp.einsum('qhgd,khd->hgqk', query_block_rows, block_keys)
        query_pos = row_beginning + jnp.arange(query_block).astype(jnp.int32)
        key_pos = row_beginning - WINDOW_LENGTH + jnp.arange(key_span).astype(jnp.int32)
        query_start = lax.dynamic_slice_in_dim(tok_start, row_beginning, query_block, 0)
        visible = (key_pos[None, :] >= query_start[:, None]) & (key_pos[None, :] <= query_pos[:, None]) & (query_pos[:, None] - key_pos[None, :] < WINDOW_LENGTH)
        scaled = raw_scores * ATTN_SCALE
        raised = jnp.where(visible[None, None], jnp.exp(scaled), 0.0)
        weights = (raised / lax.optimization_barrier(jnp.sum(raised, axis=-1, keepdims=True))).astype(jnp.bfloat16)
        mixed_vals = jnp.einsum('hgqk,khd->qhgd', weights.astype(jnp.float32), block_values)
        return mixed_vals.astype(jnp.bfloat16).reshape(query_block, QUERY_HEADS * HEAD_SIZE)
    block_starts = jnp.arange(SLAB_TOKENS // query_block).astype(jnp.int32) * query_block
    attention = lax.map(attend, block_starts).reshape(SLAB_TOKENS, QUERY_HEADS * HEAD_SIZE)

    def project_out(inputs):
        attention_rows, selected_adapter = inputs
        rank_activations = jnp.einsum('ep,epy->ey', attention_rows.astype(jnp.float32), adapter_down_output[selected_adapter].astype(jnp.float32))
        rank_lower_part = lax.optimization_barrier(rank_activations.astype(jnp.bfloat16)).astype(jnp.float32)
        return jnp.einsum('xv,xvp->xp', rank_lower_part, adapter_up_output[selected_adapter].astype(jnp.float32))
    output_terms = lax.map(project_out, (repeated_tiles(attention), repeated_tiles(adapter))).reshape(SLAB_TOKENS, MODEL_WIDTH)
    adapter_output_term = (ADAPTER_SCALE * output_terms).astype(jnp.bfloat16)
    return (attention, adapter_output_term)
```

```python
import functools
import math

import jax
import jax.numpy as jnp
import numpy as np
from jax import lax
from jax.experimental import pallas as pl
from jax.experimental.pallas import tpu as pltpu
from jax.sharding import PartitionSpec as P

HEAD_SIZE = 128
ADAPTER_RANK = 16
WINDOW_LENGTH = 1024
DOC_UNIT = 128

ADAPTER_SCALE = 2.0
ATTN_SCALE = 168.0 ** (-0.5)
ROPE_BASE = 10000.0
NORM_EPS = 1e-06
EXP2_SCALE = ATTN_SCALE * math.log2(math.e)
MASKED = -1e30
DIRECT_MOST = 4

F32 = jnp.float32
BF16 = jnp.bfloat16


def dot(a, b, dims):
    return lax.dot_general(a, b, (dims, ((), ())), preferred_element_type=F32)


def over_seq(block):
    n = lax.axis_size("seq")
    if n > DIRECT_MOST:
        return [lax.all_gather(block, "seq", axis=0)]
    got = [block]
    for k in range(1, n):
        got.append(lax.ppermute(block, "seq", [(i, (i + k) % n) for i in range(n)]))
    return [g[None] for g in got]


def slot_owner(slot):
    n = lax.axis_size("seq")
    if n > DIRECT_MOST:
        return slot
    return lax.rem(lax.axis_index("seq") - slot + n, n)


def stacked(refs, rows, columns):
    return jnp.concatenate(
        [ref[j, rows, columns] for ref in refs for j in range(ref.shape[0])], axis=0
    )


def swap_sum(value, axis, send):
    n = lax.axis_size(axis)
    low = value.astype(send)
    total = value
    for k in range(1, n):
        total = total + lax.ppermute(low, axis, [(i, (i + k) % n) for i in range(n)]).astype(F32)
    return total


def documents_of(tok, lens, rows):
    start = jnp.int32(0)
    tok_start = jnp.zeros_like(tok)
    adapter = jnp.zeros_like(tok)
    for d in range(lens.shape[0]):
        inside = tok >= start
        tok_start = jnp.where(inside, start, tok_start)
        adapter = jnp.where(inside, rows[d], adapter)
        start = start + lens[d] * DOC_UNIT
    return tok_start, adapter


def lane_tokens(first, count):
    return first + lax.broadcasted_iota(jnp.int32, (1, count), 1)


def spread(low, adapter, slots):
    return jnp.concatenate(
        [jnp.where(adapter == slot_owner(s), low, 0.0) for s in range(slots)], axis=0
    ).astype(BF16)


def select(projected, adapter, slots):
    rows = projected.shape[0] // slots
    total = jnp.zeros((rows, projected.shape[1]), F32)
    for s in range(slots):
        total = total + jnp.where(
            adapter == slot_owner(s), projected[s * rows : (s + 1) * rows], 0.0
        )
    return total


def slots_of(refs):
    return sum(ref.shape[0] for ref in refs)


def rank_in_kernel(lens, rows, hidden_t, *rest):
    parts, out = rest[:-1], rest[-1]
    width = hidden_t.shape[1]
    first = lax.axis_index("seq") * (width * pl.num_programs(0)) + pl.program_id(0) * width
    _, adapter = documents_of(lane_tokens(first, width), lens, rows)
    maps = stacked(parts, slice(None), slice(None))
    projected = dot(maps, hidden_t[...], ((1,), (0,)))
    out[...] = select(projected, adapter, slots_of(parts))


def smem():
    return pl.BlockSpec(memory_space=pltpu.SMEM)


def vmem():
    return pl.BlockSpec(memory_space=pltpu.VMEM)


def rank_in(lens, rows, hidden_t, parts):
    columns, tokens = hidden_t.shape
    block = min(256, tokens)
    return pl.pallas_call(
        rank_in_kernel,
        out_shape=jax.ShapeDtypeStruct((parts[0].shape[1], tokens), F32),
        grid=(tokens // block,),
        in_specs=[smem(), smem(), pl.BlockSpec((columns, block), lambda i: (0, i))]
        + [pl.BlockSpec(p.shape, lambda i: (0, 0, 0)) for p in parts],
        out_specs=pl.BlockSpec((parts[0].shape[1], block), lambda i: (0, i)),
        name="rank_in",
    )(lens, rows, hidden_t, *parts)


def normed_rotated(x, cosines, sines):
    factor = lax.rsqrt(jnp.mean(x * x, axis=-1, keepdims=True) + NORM_EPS)
    return (factor * (x * cosines + pltpu.roll(x, HEAD_SIZE // 2, 1) * sines)).astype(BF16)


def own_kernel(
    lens, rows, frozen_q, frozen_k, frozen_v, rank, cos_q, sin_q, cos_k, sin_k, *rest, parts_n
):
    parts = rest[:parts_n]
    q_out, acc_out, sum_out, k_s, v_s, spread_s = rest[parts_n:]
    tokens = frozen_q.shape[0]
    wide_q, wide_k = frozen_q.shape[1], frozen_k.shape[1]
    heads_q, heads_kv = wide_q // HEAD_SIZE, wide_k // HEAD_SIZE
    group = heads_q // heads_kv
    slots = slots_of(parts)
    first = lax.axis_index("seq") * tokens
    _, adapter = documents_of(lane_tokens(first, tokens), lens, rows)
    low = rank[...].astype(F32) * ADAPTER_SCALE
    r = ADAPTER_RANK
    for j in range(3):
        spread_s[j] = spread(low[j * r : (j + 1) * r], adapter, slots)
    up_q = stacked(parts, slice(0, r), slice(0, wide_q))
    up_k = stacked(parts, slice(0, r), slice(wide_q, wide_q + wide_k))
    up_v = stacked(parts, slice(0, r), slice(wide_q + wide_k, wide_q + 2 * wide_k))
    step = DOC_UNIT

    def project(i, _):
        at = pl.ds(pl.multiple_of(i * step, step), step)
        q = frozen_q[at, :].astype(F32) + dot(spread_s[0, :, at], up_q, ((0,), (0,)))
        k = frozen_k[at, :].astype(F32) + dot(spread_s[1, :, at], up_k, ((0,), (0,)))
        v = frozen_v[at, :].astype(F32) + dot(spread_s[2, :, at], up_v, ((0,), (0,)))
        for h in range(heads_q):
            head = slice(h * HEAD_SIZE, (h + 1) * HEAD_SIZE)
            q_out[at, head] = normed_rotated(q[:, head], cos_q[at, :], sin_q[at, :])
        for h in range(heads_kv):
            head = slice(h * HEAD_SIZE, (h + 1) * HEAD_SIZE)
            k_s[at, head] = normed_rotated(k[:, head], cos_k[at, :], sin_k[at, :])
            v_s[h, at, :HEAD_SIZE] = v[:, head].astype(BF16)
            v_s[h, at, HEAD_SIZE:] = jnp.ones((step, HEAD_SIZE), BF16)
        return 0

    lax.fori_loop(0, tokens // step, project, 0)

    row = lax.broadcasted_iota(jnp.int32, (group * step, step), 0) % step
    column = lax.broadcasted_iota(jnp.int32, (group * step, step), 1)
    causal = jnp.where(column <= row, 0.0, MASKED)
    for i in range(tokens // step):
        at = slice(i * step, (i + 1) * step)
        keys = (i + 1) * step
        begin, _ = documents_of(first + i * step, lens, rows)
        seen = jnp.where(lane_tokens(first, keys) >= begin, 0.0, MASKED)
        for h in range(heads_kv):
            head = slice(h * HEAD_SIZE, (h + 1) * HEAD_SIZE)
            q = jnp.concatenate(
                [
                    q_out[at, (h * group + g) * HEAD_SIZE : (h * group + g + 1) * HEAD_SIZE]
                    for g in range(group)
                ],
                axis=0,
            )
            score = dot(q, k_s[:keys, head], ((1,), (1,))) * EXP2_SCALE + seen
            edge = score[:, i * step :] + causal
            score = edge if i == 0 else jnp.concatenate([score[:, : i * step], edge], axis=1)
            weight = jnp.exp2(score).astype(BF16)
            mixed = dot(weight, v_s[h, :keys, :], ((1,), (0,)))
            for g in range(group):
                to = slice((h * group + g) * HEAD_SIZE, (h * group + g + 1) * HEAD_SIZE)
                acc_out[at, to] = mixed[g * step : (g + 1) * step, :HEAD_SIZE]
                sum_out[at, to] = mixed[g * step : (g + 1) * step, HEAD_SIZE:]


def halo_kernel(lens, rows, halo, rank, cos_k, sin_k, q_in, acc, sums, *rest, parts_n, wide_q):
    parts = rest[:parts_n]
    out, rank_out, k_s, v_s, spread_s = rest[parts_n:]
    tokens = out.shape[0]
    wide_k = halo.shape[1] // 2
    heads_q, heads_kv = wide_q // HEAD_SIZE, wide_k // HEAD_SIZE
    group = heads_q // heads_kv
    slots = slots_of(parts)
    first = lax.axis_index("seq") * tokens
    before = first - tokens
    _, adapter = documents_of(lane_tokens(before, tokens), lens, rows)
    low = rank[...].astype(F32) * ADAPTER_SCALE
    r = ADAPTER_RANK
    for j in range(2):
        spread_s[j] = spread(low[j * r : (j + 1) * r], adapter, slots)
    up_k = stacked(parts, slice(0, r), slice(wide_q, wide_q + wide_k))
    up_v = stacked(parts, slice(0, r), slice(wide_q + wide_k, wide_q + 2 * wide_k))
    step = DOC_UNIT

    def project(i, _):
        at = pl.ds(pl.multiple_of(i * step, step), step)
        k = halo[at, :wide_k].astype(F32) + dot(spread_s[0, :, at], up_k, ((0,), (0,)))
        v = halo[at, wide_k:].astype(F32) + dot(spread_s[1, :, at], up_v, ((0,), (0,)))
        for h in range(heads_kv):
            head = slice(h * HEAD_SIZE, (h + 1) * HEAD_SIZE)
            k_s[at, head] = normed_rotated(k[:, head], cos_k[at, :], sin_k[at, :])
            v_s[h, at, :HEAD_SIZE] = v[:, head].astype(BF16)
            v_s[h, at, HEAD_SIZE:] = jnp.ones((step, HEAD_SIZE), BF16)
        return 0

    lax.fori_loop(0, tokens // step, project, 0)

    row = lax.broadcasted_iota(jnp.int32, (group * step, step), 0) % step
    column = lax.broadcasted_iota(jnp.int32, (group * step, step), 1)
    beyond = jnp.where(column > row, 0.0, MASKED)
    for i in range(tokens // step):
        at = slice(i * step, (i + 1) * step)
        begin, _ = documents_of(first + i * step, lens, rows)
        seen = jnp.where(lane_tokens(before + i * step, tokens - i * step) >= begin, 0.0, MASKED)
        for h in range(heads_kv):
            head = slice(h * HEAD_SIZE, (h + 1) * HEAD_SIZE)
            q = jnp.concatenate(
                [
                    q_in[at, (h * group + g) * HEAD_SIZE : (h * group + g + 1) * HEAD_SIZE]
                    for g in range(group)
                ],
                axis=0,
            )
            score = dot(q, k_s[i * step :, head], ((1,), (1,))) * EXP2_SCALE + seen
            edge = score[:, :step] + beyond
            score = jnp.concatenate([edge, score[:, step:]], axis=1) if score.shape[1] > step else edge
            weight = jnp.exp2(score).astype(BF16)
            mixed = dot(weight, v_s[h, i * step :, :], ((1,), (0,)))
            for g in range(group):
                to = slice((h * group + g) * HEAD_SIZE, (h * group + g + 1) * HEAD_SIZE)
                part = slice(g * step, (g + 1) * step)
                total = acc[at, to] + mixed[part, :HEAD_SIZE]
                out[at, to] = (total / (sums[at, to] + mixed[part, HEAD_SIZE:])).astype(BF16)

    down = stacked(parts, slice(0, r), slice(wide_q + 2 * wide_k, 2 * wide_q + 2 * wide_k))
    _, adapter = documents_of(lane_tokens(first, tokens), lens, rows)
    projected = dot(down, out[...], ((1,), (1,)))
    rank_out[...] = select(projected, adapter, slots)


def term_kernel(lens, rows, low, *rest, begin):
    parts, out = rest[:-1], rest[-1]
    width = out.shape[1]
    first = lax.axis_index("seq") * (width * pl.num_programs(0)) + pl.program_id(0) * width
    _, adapter = documents_of(lane_tokens(first, width), lens, rows)
    wide = spread(low[...].astype(BF16).astype(F32) * ADAPTER_SCALE, adapter, slots_of(parts))
    up = stacked(parts, slice(None), slice(begin, begin + out.shape[0]))
    out[...] = dot(up, wide, ((0,), (0,))).astype(BF16)


def body(
    hidden,
    frozen_query_weight,
    frozen_key_weight,
    frozen_value_weight,
    query_norm_offset,
    key_norm_offset,
    adapter_down_input,
    adapter_up_query,
    adapter_up_key,
    adapter_up_value,
    adapter_down_output,
    adapter_up_output,
    document_lengths,
    document_adapter_row,
):
    tokens, columns = hidden.shape
    wide_q, wide_k = frozen_query_weight.shape[1], frozen_key_weight.shape[1]
    heads_kv = wide_k // HEAD_SIZE
    assert tokens == WINDOW_LENGTH
    n = lax.axis_size("seq")
    lens, rows = document_lengths, document_adapter_row[:, 0]
    r = ADAPTER_RANK

    down_in = over_seq(adapter_down_input[0].T)
    packed = jnp.concatenate(
        [
            adapter_up_query[0],
            adapter_up_key[0],
            adapter_up_value[0],
            adapter_down_output[0].T,
            adapter_up_output[0],
        ],
        axis=1,
    )
    frozen_kv = jnp.concatenate([frozen_key_weight, frozen_value_weight], axis=1)

    first = lax.axis_index("seq") * tokens
    tok = first - tokens + jnp.arange(2 * tokens, dtype=jnp.int32)
    doc_start = (jnp.cumsum(lens) - lens) * DOC_UNIT
    start = jnp.max(jnp.where(tok[:, None] >= doc_start[None, :], doc_start[None, :], 0), axis=1)
    half = HEAD_SIZE // 2
    inv_freq = (ROPE_BASE ** (-2.0 * np.arange(half) / HEAD_SIZE)).astype(np.float32)
    angle = (tok - start).astype(F32)[:, None] * np.tile(inv_freq, 2)[None, :]
    cosine, sine = jnp.cos(angle), jnp.sin(angle)
    sine = sine * np.repeat(np.array([-1.0, 1.0], np.float32), half)[None, :]
    scale_q, scale_k = 1.0 + query_norm_offset, 1.0 + key_norm_offset
    cos_q, sin_q = cosine[tokens:] * scale_q, sine[tokens:] * jnp.roll(scale_q, half)
    cos_k, sin_k = cosine * scale_k, sine * jnp.roll(scale_k, half)

    down_in, packed, frozen_kv = lax.optimization_barrier((down_in, packed, frozen_kv))
    parts = over_seq(packed)
    from_before = [(i, i + 1) for i in range(n - 1)]
    halo = lax.ppermute(frozen_kv, "seq", from_before)

    rank = rank_in(lens, rows, hidden.T, down_in)
    rank = swap_sum(rank, "rep", F32)
    rank = swap_sum(rank, "tensor", BF16).astype(BF16)
    halo_rank = lax.ppermute(rank[r:], "seq", from_before)

    slots = slots_of(parts)
    scratch = lambda count: [
        pltpu.VMEM((tokens, wide_k), BF16),
        pltpu.VMEM((heads_kv, tokens, 2 * HEAD_SIZE), BF16),
        pltpu.VMEM((count, slots * r, tokens), BF16),
    ]
    q_rot, acc, sums = pl.pallas_call(
        functools.partial(own_kernel, parts_n=len(parts)),
        out_shape=(
            jax.ShapeDtypeStruct((tokens, wide_q), BF16),
            jax.ShapeDtypeStruct((tokens, wide_q), F32),
            jax.ShapeDtypeStruct((tokens, wide_q), F32),
        ),
        in_specs=[smem(), smem()] + [vmem()] * (8 + len(parts)),
        out_specs=(vmem(), vmem(), vmem()),
        scratch_shapes=scratch(3),
        name="own_block",
    )(
        lens,
        rows,
        frozen_query_weight,
        frozen_key_weight,
        frozen_value_weight,
        rank,
        cos_q,
        sin_q,
        cos_k[tokens:],
        sin_k[tokens:],
        *parts,
    )
    attention, rank_out = pl.pallas_call(
        functools.partial(halo_kernel, parts_n=len(parts), wide_q=wide_q),
        out_shape=(
            jax.ShapeDtypeStruct((tokens, wide_q), BF16),
            jax.ShapeDtypeStruct((r, tokens), F32),
        ),
        in_specs=[smem(), smem()] + [vmem()] * (7 + len(parts)),
        out_specs=(vmem(), vmem()),
        scratch_shapes=scratch(2),
        name="halo_block",
    )(lens, rows, halo, halo_rank, cos_k[:tokens], sin_k[:tokens], q_rot, acc, sums, *parts)

    rank_out = swap_sum(rank_out, "rep", F32)
    rank_out = swap_sum(rank_out, "tensor", BF16)
    block = min(256, tokens)
    term = pl.pallas_call(
        functools.partial(term_kernel, begin=2 * wide_q + 2 * wide_k),
        out_shape=jax.ShapeDtypeStruct((columns, tokens), BF16),
        grid=(tokens // block,),
        in_specs=[smem(), smem(), pl.BlockSpec((r, block), lambda i: (0, i))]
        + [pl.BlockSpec(p.shape, lambda i: (0, 0, 0)) for p in parts],
        out_specs=pl.BlockSpec((columns, block), lambda i: (0, i)),
        name="output_term",
    )(lens, rows, rank_out, *parts)
    return (attention, term.T)


def solution(mesh):
    in_specs = (
        P(("groups", "seq"), ("tensor", "rep")),
        P(("groups", "seq"), ("tensor", "rep")),
        P(("groups", "seq"), ("tensor", "rep")),
        P(("groups", "seq"), ("tensor", "rep")),
        P(),
        P(),
        P("seq", ("tensor", "rep"), None),
        P("seq", None, ("tensor", "rep")),
        P("seq", None, ("tensor", "rep")),
        P("seq", None, ("tensor", "rep")),
        P("seq", ("tensor", "rep"), None),
        P("seq", None, ("tensor", "rep")),
        P("groups"),
        P("groups", None),
    )
    out_specs = (P(("groups", "seq"), ("tensor", "rep")), P(("groups", "seq"), ("tensor", "rep")))
    return jax.shard_map(body, mesh=mesh, in_specs=in_specs, out_specs=out_specs, check_vma=False)
```
